512 devices in a mesh: ctx: 32 (over z, x_hi, core), head: 16 (over x_lo, y).
Axes of the slice: x: 4 (x_hi: 2, x_lo: 2; x = x_hi * 2 + x_lo), y: 8, z: 8, core: 2. Of those that a mesh axis runs over, the one named last changes fastest.
Arguments:
- queries: bfloat16 [8192, 8192], P(('ctx', 'head')), may hold values from -6 to 6
- keys: bfloat16 [8192, 1024], P('ctx'), may hold values from -6 to 6
- values: bfloat16 [8192, 1024], P('ctx'), may hold values from -6 to 6
- doc_lengths: int32 [16], replicated, may hold values from 1 to 2048, 8192 in all
- slot_source: int32 [512], replicated, may hold values from 0 to 511, as said below
Outputs:
- attended: bfloat16 [8192, 8192], P('ctx', 'head')
The draws below stay inside these ranges and needn't reach their ends.
Inputs may be any that keep to these rules, and one draw needn't show every extreme that they name: `slot_source`: each piece appears in exactly one slot; a piece keeps its place within its block of 256 // 16 pieces (slot s holds a piece c with s and c equal modulo that count), and the pieces of one block of 256 // 16 go to as many different blocks of slots.
All inputs are finite; a program needn't handle non-finite values.
Results may differ from the reference program's by a relative error of at most 0.0036.
Values may be sent and summed in bfloat16 or wider, within the bound.
A program may use at most 128 MiB of HBM per device.

```python
import math
import jax
import jax.numpy as jnp
import numpy as np
from jax import lax

HD = 128
GROUP = 8
NDOCS = 16
TOK_DEV = 256
PIECE = 16
TOKENS = 8192
NPIECES = 512
DOC_MAX = 2048
QHEADS = 64
KVH = 8


def draw_queries(key, part):
    rest = jax.random.fold_in(key, 11)
    result = jnp.clip(jax.random.normal(rest, (TOKENS, QHEADS, HD), jnp.float32), -6.0, 6.0)
    return result.reshape(TOKENS, QHEADS * HD).astype(jnp.bfloat16)


def draw_keys(key, part):
    rest = jax.random.fold_in(key, 13)
    result = jnp.clip(jax.random.normal(rest, (TOKENS, KVH, HD), jnp.float32), -6.0, 6.0)
    return result.reshape(TOKENS, KVH * HD).astype(jnp.bfloat16)


def draw_slot_source(key, part):
    blocks = TOKENS // TOK_DEV
    per_block = TOK_DEV // PIECE
    order = jax.random.permutation(jax.random.fold_in(key, 3), blocks).astype(jnp.int32)
    inverse = jnp.zeros((blocks,), jnp.int32).at[order].set(jnp.arange(blocks, dtype=jnp.int32))
    slots = jnp.arange(blocks * per_block, dtype=jnp.int32)
    owner = slots // per_block
    place = slots % per_block
    source_block = (inverse[owner] - place) % blocks
    return (source_block * per_block + place).astype(jnp.int32)


def shard_levels(rng, dims, cuts, least, high):
    loudness, own = 1.0, jax.random.fold_in(rng, 6)
    for dim, shards_of in cuts:
        heights = jnp.exp(jax.random.uniform(jax.random.fold_in(own, dim), (shards_of,), jnp.float32, least / len(cuts), high / len(cuts)))
        loudness = loudness * jnp.repeat(heights, dims[dim] // shards_of).reshape([-1 if axis == dim else 1 for axis in range(len(dims))])
    return loudness


def profile(count, total, most, slope):
    loads = [(1 << 20) // math.isqrt(grade ** slope) + 1 for grade in range(2, count + 1)]
    surplus, given = total - most - (count - 1), [1] * (count - 1)
    while surplus > 0:
        candidates = [i for i in range(count - 1) if given[i] < most]
        mass, budget = sum([loads[i] for i in candidates]), surplus
        for i in candidates:
            more = min(most - given[i], max(1, budget * loads[i] // mass), surplus)
            given[i] = given[i] + more
            surplus = surplus - more
    return np.array([most] + given)


def ragged(own_key, count, total, limit, skew):
    if count == 2:
        one = jax.random.randint(own_key, (), max(1, total - limit), min(limit, total - 1) + 1)
        return jnp.stack([one, total - one])
    sizes = jnp.asarray(profile(count, total, limit, skew), jnp.int32)
    pairs = (count - 1) // 2
    giver, taker = sizes[1:1 + 2 * pairs:2], sizes[2:2 + 2 * pairs:2]
    slack = jnp.minimum(giver - 1, limit - taker)
    passed = jax.random.randint(jax.random.fold_in(own_key, 1), (pairs,), 0, 1 << 20) % (slack + 1)
    sizes = sizes.at[1:1 + 2 * pairs:2].set(giver - passed).at[2:2 + 2 * pairs:2].set(taker + passed)
    return sizes[jax.random.permutation(jax.random.fold_in(own_key, 2), count)]


def gaussian(own_key, shape, deviation, limit, split=(), held_as=jnp.bfloat16):
    values = jax.random.normal(own_key, shape, jnp.float32) * deviation
    if len(split) > 0:
        values = shard_levels(own_key, shape, split, -0.22, 0.18) * values
    return jnp.clip(values, min=-limit, max=limit).astype(held_as)


def setup_inputs(seed: int = 0) -> dict:
    key_of = jax.random.split(jax.random.key(seed), 6)
    queries = draw_queries(jax.random.fold_in(key_of[5], 71), 0)
    keys = draw_keys(jax.random.fold_in(key_of[5], 71), 0)
    values = gaussian(key_of[2], (TOKENS, KVH * HD), 1.0, 6.0, ((0, 32),))
    doc_lengths = ragged(key_of[3], NDOCS, TOKENS, DOC_MAX, 2).astype(jnp.int32)
    slot_source = draw_slot_source(jax.random.fold_in(key_of[5], 71), 0)
    return {"queries": queries, "keys": keys, "values": values, "doc_lengths": doc_lengths, "slot_source": slot_source}


def reference(queries, keys, values, doc_lengths, slot_source):
    window = DOC_MAX + PIECE
    ends = jnp.cumsum(doc_lengths).astype(jnp.int32)
    scale = 1.0 / (HD ** 0.5)
    q_all = queries.reshape(TOKENS, QHEADS, HD)
    k_all = keys.reshape(TOKENS, KVH, HD)
    v_all = values.reshape(TOKENS, KVH, HD)

    def attend_piece(source):
        q_start = (source * PIECE).astype(jnp.int32)
        k_start = jnp.clip(q_start + PIECE - window, 0, TOKENS - window).astype(jnp.int32)
        query = lax.dynamic_slice_in_dim(q_all, q_start, PIECE, 0).astype(jnp.float32).reshape(PIECE, KVH, GROUP, HD)
        key_rows = lax.dynamic_slice_in_dim(k_all, k_start, window, 0).astype(jnp.float32)
        value_rows = lax.dynamic_slice_in_dim(v_all, k_start, window, 0).astype(jnp.float32)
        q_pos = q_start + jnp.arange(PIECE, dtype=jnp.int32)
        k_pos = k_start + jnp.arange(window, dtype=jnp.int32)
        q_doc = jnp.sum((ends[None, :] <= q_pos[:, None]).astype(jnp.int32), axis=1)
        k_doc = jnp.sum((ends[None, :] <= k_pos[:, None]).astype(jnp.int32), axis=1)
        allowed = (q_doc[:, None] == k_doc[None, :]) & (k_pos[None, :] <= q_pos[:, None])
        score = jnp.einsum("qhgd,khd->hgqk", query, key_rows) * scale
        score = jnp.where(allowed, score, -1e30)
        peak = jnp.max(score, axis=-1, keepdims=True)
        weight = jnp.where(allowed, jnp.exp(score - peak), 0.0)
        total = jnp.sum(weight, axis=-1)
        rounded = lax.optimization_barrier(weight.astype(jnp.bfloat16)).astype(jnp.float32)
        mixed = jnp.einsum("hgqk,khd->hgqd", rounded, value_rows)
        result = (mixed / total[..., None]).astype(jnp.bfloat16)
        return jnp.transpose(result, (2, 0, 1, 3)).reshape(PIECE, QHEADS * HD)

    pieces = lax.map(attend_piece, slot_source)
    return pieces.reshape(NPIECES * PIECE, QHEADS * HD)
```

```python
import functools
import math

import jax
import jax.numpy as jnp
from jax import lax
from jax.experimental import pallas as pl
from jax.experimental.pallas import tpu as pltpu
from jax.sharding import PartitionSpec as P

HD = 128
GROUP = 8
DOC_MAX = 2048
MASKED = -1e30
MESH = pl.DeviceIdType.MESH


def kernel(
    nctx, nhead, win, chunk,
    pick, slots, lengths, q_ref, k_ref, v_ref, o_ref,
    qbuf, kwin, vwin, bias, obuf, sbuf, rbuf,
    own_sem, q_send, q_recv, kv_send, kv_recv, f_send, f_recv, o_send, o_recv,
):
    ctx = lax.axis_index("ctx")
    head = lax.axis_index("head")
    piece, width = q_ref.shape[0], q_ref.shape[1] // nhead
    rows = k_ref.shape[0]
    count = rows // piece
    heads = width // HD
    chips = nctx // 2
    reach = win // 2
    core = lax.rem(ctx, 2)
    chip = ctx // 2
    sibling = chip * 2 + 1 - core

    barrier = pltpu.get_barrier_semaphore()

    @pl.loop(1, nctx)
    def _(t):
        pl.semaphore_signal(barrier, device_id=(lax.rem(ctx + t, nctx), head), device_id_type=MESH)

    @pl.loop(1, nhead)
    def _(t):
        pl.semaphore_signal(barrier, device_id=(ctx, lax.rem(head + t, nhead)), device_id_type=MESH)

    pl.semaphore_wait(barrier, nctx + nhead - 2)

    kv_cols = pl.ds(pl.multiple_of(((head * heads) // GROUP) * HD, HD), HD)

    def block(index):
        return pl.ds(pl.multiple_of(index * rows, rows), rows)

    def kv_copy(which, step):
        src = (k_ref, v_ref)[which]
        dst = (kwin, vwin)[which]
        return pltpu.make_async_remote_copy(
            src_ref=src.at[:, kv_cols],
            dst_ref=dst.at[block((reach - step) * 2 + core)],
            send_sem=kv_send.at[which, step],
            recv_sem=kv_recv.at[which, step],
            device_id=(lax.rem(chip + step, chips) * 2 + core, head),
            device_id_type=MESH,
        )

    def pass_copy(which, step):
        dst = (kwin, vwin)[which]
        spot = dst.at[block((reach - step) * 2 + core)]
        return pltpu.make_async_remote_copy(
            src_ref=spot,
            dst_ref=spot,
            send_sem=f_send.at[which, step],
            recv_sem=f_recv.at[which, step],
            device_id=(sibling, head),
            device_id_type=MESH,
        )

    def own_copy(which):
        src = (k_ref, v_ref)[which]
        dst = (kwin, vwin)[which]
        return pltpu.make_async_copy(src.at[:, kv_cols], dst.at[block(reach * 2 + core)], own_sem.at[which])

    for step in range(1, reach + 1):
        for which in range(2):
            kv_copy(which, step).start()
    for which in range(2):
        own_copy(which).start()

    def q_copy(t):
        peer = lax.rem(head + t, nhead)
        return pltpu.make_async_remote_copy(
            src_ref=q_ref.at[:, pl.ds(pl.multiple_of(peer * width, width), width)],
            dst_ref=qbuf.at[head],
            send_sem=q_send.at[t],
            recv_sem=q_recv.at[t],
            device_id=(ctx, peer),
            device_id_type=MESH,
        )

    @pl.loop(1, nhead)
    def _(t):
        q_copy(t).start()

    q_own = pltpu.make_async_copy(
        q_ref.at[:, pl.ds(pl.multiple_of(head * width, width), width)], qbuf.at[head], own_sem.at[2]
    )
    q_own.start()

    keys = (win + 1) * rows
    for lower in range(0, rows, chunk):
        line = lower + lax.broadcasted_iota(jnp.int32, (chunk, 1), 0)
        position = ctx * rows + line
        start = jnp.zeros((chunk, 1), jnp.int32)
        end = jnp.int32(0)
        for j in range(lengths.shape[0]):
            end = end + lengths[j]
            start = jnp.where(position >= end, end, start)
        start = start - (ctx - win) * rows
        for col in range(0, keys, rows):
            at = col + lax.broadcasted_iota(jnp.int32, (chunk, rows), 1)
            allowed = (at >= start) & (at <= win * rows + line)
            bias[lower : lower + chunk, col : col + rows] = jnp.where(allowed, 0.0, MASKED)

    for which in range(2):
        own_copy(which).wait()
        pass_copy(which, 0).start()
    for step in range(1, reach + 1):
        for which in range(2):
            kv_copy(which, step).wait_recv()
            pass_copy(which, step).start()
    q_own.wait()

    @pl.loop(1, nhead)
    def _(t):
        q_copy(t).wait_recv()

    for step in range(reach + 1):
        for which in range(2):
            pass_copy(which, step).wait_recv()

    seen = pl.ds(pl.multiple_of(core * rows, rows), keys)
    factor = math.log2(math.e) / HD**0.5

    def o_copy(h, t):
        owner = lax.rem(ctx + t, nctx)
        return pltpu.make_async_remote_copy(
            src_ref=sbuf.at[h, owner],
            dst_ref=rbuf.at[h, ctx],
            send_sem=o_send.at[h],
            recv_sem=o_recv.at[h],
            device_id=(owner, head),
            device_id_type=MESH,
        )

    @pl.loop(0, heads)
    def _(h):
        cols = pl.ds(pl.multiple_of(h * HD, HD), HD)
        for lower in range(0, rows, chunk):
            pieces = pl.ds(lower // piece, chunk // piece)
            query = qbuf[pieces, :, cols].reshape(chunk, HD)
            score = lax.dot_general(
                query, kwin[seen], (((1,), (1,)), ((), ())), preferred_element_type=jnp.float32
            )
            score = score + bias[lower : lower + chunk, :]
            peak = jnp.max(score, axis=-1, keepdims=True)
            weight = jnp.exp2((score - peak) * factor)
            total = jnp.sum(weight, axis=-1, keepdims=True)
            mixed = jnp.dot(
                weight.astype(jnp.bfloat16), vwin[seen], preferred_element_type=jnp.float32
            )
            mixed = mixed * (1.0 / total)
            obuf[h, pieces] = mixed.astype(jnp.bfloat16).reshape(chunk // piece, piece, HD)

        @pl.loop(0, nctx)
        def _(owner):
            sbuf[h, owner] = obuf[h, pick[owner]]

        @pl.loop(1, nctx)
        def _(t):
            o_copy(h, t).start()

        rbuf[h, ctx] = sbuf[h, ctx]

    for h in range(heads):
        arrived = rbuf.at[h, pl.ds(0, nctx - 1)]
        pltpu.make_async_copy(arrived, arrived, o_recv.at[h]).wait()
    for h in range(heads):
        for place in range(count):
            source = slots[ctx * count + place] // count
            o_ref[place * piece : (place + 1) * piece, h * HD : (h + 1) * HD] = rbuf[h, source]

    for h in range(heads):
        left = sbuf.at[h, pl.ds(0, nctx - 1)]
        pltpu.make_async_copy(left, left, o_send.at[h]).wait()

    @pl.loop(1, nhead)
    def _(t):
        q_copy(t).wait_send()

    for which in range(2):
        for step in range(1, reach + 1):
            kv_copy(which, step).wait_send()
        for step in range(reach + 1):
            pass_copy(which, step).wait_send()


def solution(mesh):
    nctx, nhead = mesh.shape["ctx"], mesh.shape["head"]

    def local(queries, keys, values, doc_lengths, slot_source):
        piece, width = queries.shape[0], queries.shape[1] // nhead
        rows = keys.shape[0]
        heads = width // HD
        win = DOC_MAX // rows
        chunk = min(128, rows)
        places = jnp.arange(nhead, dtype=jnp.int32)[None, :]
        mine = slot_source.reshape(nctx, nhead) == lax.axis_index("ctx") * nhead + places
        pick = jnp.sum(jnp.where(mine, places, 0), axis=1)
        dma = pltpu.SemaphoreType.DMA
        return pl.pallas_call(
            functools.partial(kernel, nctx, nhead, win, chunk),
            out_shape=jax.ShapeDtypeStruct((rows, width), jnp.bfloat16),
            in_specs=[pl.BlockSpec(memory_space=pltpu.SMEM)] * 3 + [pl.BlockSpec(memory_space=pl.ANY)] * 3,
            out_specs=pl.BlockSpec(memory_space=pltpu.VMEM),
            scratch_shapes=[
                pltpu.VMEM((rows // piece, piece, width), jnp.bfloat16),
                pltpu.VMEM(((win + 2) * rows, HD), jnp.bfloat16),
                pltpu.VMEM(((win + 2) * rows, HD), jnp.bfloat16),
                pltpu.VMEM((rows, (win + 1) * rows), jnp.float32),
                pltpu.VMEM((heads, rows // piece, piece, HD), jnp.bfloat16),
                pltpu.VMEM((heads, nctx, piece, HD), jnp.bfloat16),
                pltpu.VMEM((heads, nctx, piece, HD), jnp.bfloat16),
                dma((3,)),
                dma((nhead,)),
                dma((nhead,)),
                dma((2, win // 2 + 1)),
                dma((2, win // 2 + 1)),
                dma((2, win // 2 + 1)),
                dma((2, win // 2 + 1)),
                dma((heads,)),
                dma((heads,)),
            ],
            compiler_params=pltpu.CompilerParams(
                collective_id=0, has_side_effects=True, vmem_limit_bytes=56 * 2**20
            ),
        )(pick, slot_source, doc_lengths, queries, keys, values)

    return jax.shard_map(
        local,
        mesh=mesh,
        in_specs=(P(("ctx", "head"), None), P("ctx", None), P("ctx", None), P(), P()),
        out_specs=P("ctx", "head"),
        check_vma=False,
    )
```

```python
import functools
import math

import jax
import jax.numpy as jnp
from jax import lax
from jax.experimental import pallas as pl
from jax.experimental.pallas import tpu as pltpu
from jax.sharding import PartitionSpec as P

HD = 128
GROUP = 8
DOC_MAX = 2048
MASKED = -1e30
MESH = pl.DeviceIdType.MESH


def kernel(
    nctx, nhead, win, chunk,
    pick, slots, lengths, q_ref, k_ref, v_ref, o_ref,
    qbuf, kvwin, bias, obuf, sbuf, rbuf,
    own_sem, q_send, q_recv, kv_send, kv_recv, f_send, f_recv, o_send, o_recv,
):
    ctx = lax.axis_index("ctx")
    head = lax.axis_index("head")
    piece, width = q_ref.shape[0], q_ref.shape[1] // nhead
    rows = k_ref.shape[0]
    count = rows // piece
    heads = width // HD
    deep = nctx // 4
    z, xh, core = ctx // 4, lax.rem(ctx // 2, 2), lax.rem(ctx, 2)
    above = (lax.rem(z + 1, deep) * 4 + xh * 2 + core, head)
    opposite = (z * 4 + (1 - xh) * 2 + core, head)
    sibling = (z * 4 + xh * 2 + 1 - core, head)

    barrier = pltpu.get_barrier_semaphore()

    @pl.loop(1, nctx)
    def _(t):
        pl.semaphore_signal(barrier, device_id=(lax.rem(ctx + t, nctx), head), device_id_type=MESH)

    @pl.loop(1, nhead)
    def _(t):
        pl.semaphore_signal(barrier, device_id=(ctx, lax.rem(head + t, nhead)), device_id_type=MESH)

    pl.semaphore_wait(barrier, nctx + nhead - 2)

    kv_cols = pl.ds(pl.multiple_of(((head * heads) // GROUP) * HD, HD), HD)

    def part(which, step):
        return kvwin.at[which, pl.ds(pl.multiple_of((step * 2 + core) * rows, rows), rows)]

    def own_copy(which):
        return pltpu.make_async_copy((k_ref, v_ref)[which].at[:, kv_cols], part(which, 4), own_sem.at[which])

    routes = [
        (above, None, 2),
        (above, 2, 0),
        (opposite, 2, 1 + 2 * xh),
        (opposite, (1 - xh) * 4, 3 - 2 * xh),
    ]

    def kv_copy(i, which):
        to, source, target = routes[i]
        src = (k_ref, v_ref)[which].at[:, kv_cols] if source is None else part(which, source)
        return pltpu.make_async_remote_copy(
            src_ref=src,
            dst_ref=part(which, target),
            send_sem=kv_send.at[i, which],
            recv_sem=kv_recv.at[i, which],
            device_id=to,
            device_id_type=MESH,
        )

    given = [4, 2, 0, 3 - 2 * xh, 1 + 2 * xh]

    def pass_copy(i, which):
        where = part(which, given[i])
        return pltpu.make_async_remote_copy(
            src_ref=where,
            dst_ref=where,
            send_sem=f_send.at[i, which],
            recv_sem=f_recv.at[i, which],
            device_id=sibling,
            device_id_type=MESH,
        )

    for which in range(2):
        kv_copy(0, which).start()
    for which in range(2):
        own_copy(which).start()

    def q_copy(t):
        peer = lax.rem(head + t, nhead)
        return pltpu.make_async_remote_copy(
            src_ref=q_ref.at[:, pl.ds(pl.multiple_of(peer * width, width), width)],
            dst_ref=qbuf.at[head],
            send_sem=q_send.at[t],
            recv_sem=q_recv.at[t],
            device_id=(ctx, peer),
            device_id_type=MESH,
        )

    @pl.loop(1, nhead)
    def _(t):
        q_copy(t).start()

    q_own = pltpu.make_async_copy(
        q_ref.at[:, pl.ds(pl.multiple_of(head * width, width), width)], qbuf.at[head], own_sem.at[2]
    )
    q_own.start()

    keys = (win + 1) * rows
    for lower in range(0, rows, chunk):
        line = lower + lax.broadcasted_iota(jnp.int32, (chunk, 1), 0)
        position = ctx * rows + line
        start = jnp.zeros((chunk, 1), jnp.int32)
        end = jnp.int32(0)
        for j in range(lengths.shape[0]):
            end = end + lengths[j]
            start = jnp.where(position >= end, end, start)
        start = start - (ctx - win) * rows
        for col in range(0, keys, rows):
            at = col + lax.broadcasted_iota(jnp.int32, (chunk, rows), 1)
            allowed = (at >= start) & (at <= win * rows + line)
            bias[lower : lower + chunk, col : col + rows] = jnp.where(allowed, 0.0, MASKED)

    for which in range(2):
        own_copy(which).wait()
        pass_copy(0, which).start()
    for which in range(2):
        kv_copy(0, which).wait_recv()
        kv_copy(1, which).start()
        kv_copy(2, which).start()
        pass_copy(1, which).start()
    for which in range(2):
        kv_copy(1, which).wait_recv()
        kv_copy(3, which).start()
        pass_copy(2, which).start()
    for i in (2, 3):
        for which in range(2):
            kv_copy(i, which).wait_recv()
            pass_copy(i + 1, which).start()
    q_own.wait()

    @pl.loop(1, nhead)
    def _(t):
        q_copy(t).wait_recv()

    for i in range(5):
        for which in range(2):
            pass_copy(i, which).wait_recv()

    seen = pl.ds(pl.multiple_of(core * rows, rows), keys)
    factor = math.log2(math.e) / HD**0.5

    def o_copy(h, t):
        owner = lax.rem(ctx + t, nctx)
        return pltpu.make_async_remote_copy(
            src_ref=sbuf.at[h, owner],
            dst_ref=rbuf.at[h, ctx],
            send_sem=o_send.at[h],
            recv_sem=o_recv.at[h],
            device_id=(owner, head),
            device_id_type=MESH,
        )

    @pl.loop(0, heads)
    def _(h):
        cols = pl.ds(pl.multiple_of(h * HD, HD), HD)
        for lower in range(0, rows, chunk):
            pieces = pl.ds(lower // piece, chunk // piece)
            query = qbuf[pieces, :, cols].reshape(chunk, HD)
            score = lax.dot_general(
                query, kvwin[0, seen], (((1,), (1,)), ((), ())), preferred_element_type=jnp.float32
            )
            score = score + bias[lower : lower + chunk, :]
            peak = jnp.max(score, axis=-1, keepdims=True)
            weight = jnp.exp2((score - peak) * factor)
            total = jnp.sum(weight, axis=-1, keepdims=True)
            mixed = jnp.dot(
                weight.astype(jnp.bfloat16), kvwin[1, seen], preferred_element_type=jnp.float32
            )
            mixed = mixed * (1.0 / total)
            obuf[h, pieces] = mixed.astype(jnp.bfloat16).reshape(chunk // piece, piece, HD)

        @pl.loop(0, nctx)
        def _(owner):
            sbuf[h, owner] = obuf[h, pick[owner]]

        @pl.loop(1, nctx)
        def _(t):
            o_copy(h, t).start()

        rbuf[h, ctx] = sbuf[h, ctx]

    def o_waits(buffer, sem):
        for h in range(heads):
            moved = buffer.at[h, pl.ds(0, nctx - 1)]
            pltpu.make_async_copy(moved, moved, sem.at[h]).wait()

    o_waits(rbuf, o_recv)
    for h in range(heads):
        for place in range(count):
            source = slots[ctx * count + place] // count
            o_ref[place * piece : (place + 1) * piece, h * HD : (h + 1) * HD] = rbuf[h, source]

    o_waits(sbuf, o_send)

    @pl.loop(1, nhead)
    def _(t):
        q_copy(t).wait_send()

    for which in range(2):
        for i in range(4):
            kv_copy(i, which).wait_send()
        for i in range(5):
            pass_copy(i, which).wait_send()


def solution(mesh):
    nctx, nhead = mesh.shape["ctx"], mesh.shape["head"]

    def local(queries, keys, values, doc_lengths, slot_source):
        piece, width = queries.shape[0], queries.shape[1] // nhead
        rows = keys.shape[0]
        heads = width // HD
        win = DOC_MAX // rows
        chunk = min(128, rows)
        places = jnp.arange(nhead, dtype=jnp.int32)[None, :]
        mine = slot_source.reshape(nctx, nhead) == lax.axis_index("ctx") * nhead + places
        pick = jnp.sum(jnp.where(mine, places, 0), axis=1)
        dma = pltpu.SemaphoreType.DMA
        return pl.pallas_call(
            functools.partial(kernel, nctx, nhead, win, chunk),
            out_shape=jax.ShapeDtypeStruct((rows, width), jnp.bfloat16),
            in_specs=[pl.BlockSpec(memory_space=pltpu.SMEM)] * 3 + [pl.BlockSpec(memory_space=pl.ANY)] * 3,
            out_specs=pl.BlockSpec(memory_space=pltpu.VMEM),
            scratch_shapes=[
                pltpu.VMEM((rows // piece, piece, width), jnp.bfloat16),
                pltpu.VMEM((2, (win + 2) * rows, HD), jnp.bfloat16),
                pltpu.VMEM((rows, (win + 1) * rows), jnp.float32),
                pltpu.VMEM((heads, rows // piece, piece, HD), jnp.bfloat16),
                pltpu.VMEM((heads, nctx, piece, HD), jnp.bfloat16),
                pltpu.VMEM((heads, nctx, piece, HD), jnp.bfloat16),
                dma((3,)),
                dma((nhead,)),
                dma((nhead,)),
                dma((4, 2)),
                dma((4, 2)),
                dma((5, 2)),
                dma((5, 2)),
                dma((heads,)),
                dma((heads,)),
            ],
            compiler_params=pltpu.CompilerParams(
                collective_id=0, has_side_effects=True, vmem_limit_bytes=56 * 2**20
            ),
        )(pick, slot_source, doc_lengths, queries, keys, values)

    return jax.shard_map(
        local,
        mesh=mesh,
        in_specs=(P(("ctx", "head"), None), P("ctx", None), P("ctx", None), P(), P()),
        out_specs=P("ctx", "head"),
        check_vma=False,
    )
```

```python
import functools
import math

import jax
import jax.numpy as jnp
from jax import lax
from jax.experimental import pallas as pl
from jax.experimental.pallas import tpu as pltpu
from jax.sharding import PartitionSpec as P

HD = 128
GROUP = 8
DOC_MAX = 2048
MASKED = -1e30
CUTS = 2
MESH = pl.DeviceIdType.MESH


def turn(t, n):
    side = (n - t + 1) // 2
    return jnp.where((n - t) % 2 == 1, side, n - side)


def kernel(
    nctx, nhead, win, chunk,
    slots, table, lengths, q_ref, k_ref, v_ref, o_ref,
    qbuf, kvwin, bias, obuf, sbuf, rbuf, chosen, pick,
    own_sem, q_send, q_recv, kv_send, kv_recv, f_send, f_recv, o_send, o_recv,
):
    ctx = lax.axis_index("ctx")
    head = lax.axis_index("head")
    piece, width = q_ref.shape[0], q_ref.shape[1] // nhead
    rows = k_ref.shape[0]
    count = rows // piece
    heads = width // HD
    deep = nctx // 4
    z, xh, core = ctx // 4, lax.rem(ctx // 2, 2), lax.rem(ctx, 2)
    above = (lax.rem(z + 1, deep) * 4 + xh * 2 + core, head)
    opposite = (z * 4 + (1 - xh) * 2 + core, head)
    sibling = (z * 4 + xh * 2 + 1 - core, head)

    barrier = pltpu.get_barrier_semaphore()

    @pl.loop(1, nctx)
    def _(t):
        pl.semaphore_signal(barrier, device_id=(lax.rem(ctx + t, nctx), head), device_id_type=MESH)

    @pl.loop(1, nhead)
    def _(t):
        pl.semaphore_signal(barrier, device_id=(ctx, lax.rem(head + t, nhead)), device_id_type=MESH)

    pl.semaphore_wait(barrier, nctx + nhead - 2)

    kv_cols = pl.ds(pl.multiple_of(((head * heads) // GROUP) * HD, HD), HD)

    cut = rows // CUTS
    parts = range(2 * CUTS)

    def part(n, step):
        return kvwin.at[n // CUTS, pl.ds(pl.multiple_of((step * 2 + core) * rows + n % CUTS * cut, cut), cut)]

    def block(n):
        return (k_ref, v_ref)[n // CUTS].at[pl.ds(n % CUTS * cut, cut), kv_cols]

    def own_copy(n):
        return pltpu.make_async_copy(block(n), part(n, 4), own_sem.at[n])

    routes = [
        (above, None, 2),
        (above, 2, 0),
        (opposite, 2, 1 + 2 * xh),
        (opposite, (1 - xh) * 4, 3 - 2 * xh),
    ]

    def kv_copy(i, n):
        to, source, target = routes[i]
        src = block(n) if source is None else part(n, source)
        return pltpu.make_async_remote_copy(
            src_ref=src,
            dst_ref=part(n, target),
            send_sem=kv_send.at[i, n],
            recv_sem=kv_recv.at[i, n],
            device_id=to,
            device_id_type=MESH,
        )

    given = [4, 2, 0, 3 - 2 * xh, 1 + 2 * xh]

    def pass_copy(i, n):
        where = part(n, given[i])
        return pltpu.make_async_remote_copy(
            src_ref=where,
            dst_ref=where,
            send_sem=f_send.at[i, n],
            recv_sem=f_recv.at[i, n],
            device_id=sibling,
            device_id_type=MESH,
        )

    for n in parts:
        kv_copy(0, n).start()
    for n in parts:
        own_copy(n).start()

    def q_copy(t):
        peer = lax.rem(head + t, nhead)
        return pltpu.make_async_remote_copy(
            src_ref=q_ref.at[:, pl.ds(pl.multiple_of(peer * width, width), width)],
            dst_ref=qbuf.at[head],
            send_sem=q_send.at[t],
            recv_sem=q_recv.at[t],
            device_id=(ctx, peer),
            device_id_type=MESH,
        )

    @pl.loop(1, nhead)
    def _(t):
        q_copy(t).start()

    q_own = pltpu.make_async_copy(
        q_ref.at[:, pl.ds(pl.multiple_of(head * width, width), width)], qbuf.at[head], own_sem.at[2 * CUTS]
    )
    q_own.start()

    lanes = lax.broadcasted_iota(jnp.int32, table.shape, 1) % count
    found = jnp.where(table[...] == ctx * count + lanes, lanes, 0)
    shift = count // 2
    while shift:
        found = found + pltpu.roll(found, table.shape[1] - shift, 1)
        shift //= 2
    chosen[...] = found
    pick_copy = pltpu.make_async_copy(chosen, pick, own_sem.at[2 * CUTS + 1])
    pick_copy.start()
    across = table.shape[1] // count

    keys = (win + 1) * rows
    for lower in range(0, rows, chunk):
        line = lower + lax.broadcasted_iota(jnp.int32, (chunk, 1), 0)
        position = ctx * rows + line
        start = jnp.zeros((chunk, 1), jnp.int32)
        end = jnp.int32(0)
        for j in range(lengths.shape[0]):
            end = end + lengths[j]
            start = jnp.where(position >= end, end, start)
        start = start - (ctx - win) * rows
        for col in range(0, keys, rows):
            at = col + lax.broadcasted_iota(jnp.int32, (chunk, rows), 1)
            allowed = (at >= start) & (at <= win * rows + line)
            bias[lower : lower + chunk, col : col + rows] = jnp.where(allowed, 0.0, MASKED)

    for n in parts:
        own_copy(n).wait()
        pass_copy(0, n).start()
    for n in parts:
        kv_copy(0, n).wait_recv()
        kv_copy(1, n).start()
        kv_copy(2, n).start()
        pass_copy(1, n).start()
    for n in parts:
        kv_copy(1, n).wait_recv()
        kv_copy(3, n).start()
        pass_copy(2, n).start()
    for i in (2, 3):
        for n in parts:
            kv_copy(i, n).wait_recv()
            pass_copy(i + 1, n).start()
    q_own.wait()

    @pl.loop(1, nhead)
    def _(t):
        q_copy(t).wait_recv()

    for i in range(5):
        for n in parts:
            pass_copy(i, n).wait_recv()

    pick_copy.wait()
    seen = pl.ds(pl.multiple_of(core * rows, rows), keys)
    factor = math.log2(math.e) / HD**0.5

    def o_copy(h, t):
        owner = lax.rem(ctx + t, nctx)
        return pltpu.make_async_remote_copy(
            src_ref=sbuf.at[h, owner],
            dst_ref=rbuf.at[h, ctx],
            send_sem=o_send.at[h],
            recv_sem=o_recv.at[h],
            device_id=(owner, head),
            device_id_type=MESH,
        )

    @pl.loop(0, heads)
    def _(h):
        cols = pl.ds(pl.multiple_of(h * HD, HD), HD)
        for lower in range(0, rows, chunk):
            pieces = pl.ds(lower // piece, chunk // piece)
            query = qbuf[pieces, :, cols].reshape(chunk, HD)
            score = lax.dot_general(
                query, kvwin[0, seen], (((1,), (1,)), ((), ())), preferred_element_type=jnp.float32
            )
            score = score + bias[lower : lower + chunk, :]
            peak = jnp.max(score, axis=-1, keepdims=True)
            weight = jnp.exp2((score - peak) * factor)
            total = jnp.sum(weight, axis=-1, keepdims=True)
            mixed = jnp.dot(
                weight.astype(jnp.bfloat16), kvwin[1, seen], preferred_element_type=jnp.float32
            )
            mixed = mixed * (1.0 / total)
            obuf[h, pieces] = mixed.astype(jnp.bfloat16).reshape(chunk // piece, piece, HD)

        @pl.loop(0, nctx)
        def _(owner):
            sbuf[h, owner] = obuf[h, pick[owner // across, owner % across * count]]

        @pl.loop(1, nctx)
        def _(t):
            o_copy(h, turn(t, nctx)).start()

        rbuf[h, ctx] = sbuf[h, ctx]

    def o_waits(buffer, sem):
        for h in range(heads):
            moved = buffer.at[h, pl.ds(0, nctx - 1)]
            pltpu.make_async_copy(moved, moved, sem.at[h]).wait()

    o_waits(rbuf, o_recv)
    for h in range(heads):
        for place in range(count):
            source = slots[ctx * count + place] // count
            o_ref[place * piece : (place + 1) * piece, h * HD : (h + 1) * HD] = rbuf[h, source]

    o_waits(sbuf, o_send)

    @pl.loop(1, nhead)
    def _(t):
        q_copy(t).wait_send()

    for n in parts:
        for i in range(4):
            kv_copy(i, n).wait_send()
        for i in range(5):
            pass_copy(i, n).wait_send()


def solution(mesh):
    nctx, nhead = mesh.shape["ctx"], mesh.shape["head"]

    def local(queries, keys, values, doc_lengths, slot_source):
        piece, width = queries.shape[0], queries.shape[1] // nhead
        rows = keys.shape[0]
        heads = width // HD
        win = DOC_MAX // rows
        chunk = min(128, rows)
        table = slot_source.reshape(-1, min(128, slot_source.shape[0]))
        dma = pltpu.SemaphoreType.DMA
        return pl.pallas_call(
            functools.partial(kernel, nctx, nhead, win, chunk),
            out_shape=jax.ShapeDtypeStruct((rows, width), jnp.bfloat16),
            in_specs=[
                pl.BlockSpec(memory_space=pltpu.SMEM),
                pl.BlockSpec(memory_space=pltpu.VMEM),
                pl.BlockSpec(memory_space=pltpu.SMEM),
            ]
            + [pl.BlockSpec(memory_space=pl.ANY)] * 3,
            out_specs=pl.BlockSpec(memory_space=pltpu.VMEM),
            scratch_shapes=[
                pltpu.VMEM((rows // piece, piece, width), jnp.bfloat16),
                pltpu.VMEM((2, (win + 2) * rows, HD), jnp.bfloat16),
                pltpu.VMEM((rows, (win + 1) * rows), jnp.float32),
                pltpu.VMEM((heads, rows // piece, piece, HD), jnp.bfloat16),
                pltpu.VMEM((heads, nctx, piece, HD), jnp.bfloat16),
                pltpu.VMEM((heads, nctx, piece, HD), jnp.bfloat16),
                pltpu.VMEM(table.shape, jnp.int32),
                pltpu.SMEM(table.shape, jnp.int32),
                dma((2 * CUTS + 2,)),
                dma((nhead,)),
                dma((nhead,)),
                dma((4, 2 * CUTS)),
                dma((4, 2 * CUTS)),
                dma((5, 2 * CUTS)),
                dma((5, 2 * CUTS)),
                dma((heads,)),
                dma((heads,)),
            ],
            compiler_params=pltpu.CompilerParams(
                collective_id=0, has_side_effects=True, vmem_limit_bytes=56 * 2**20
            ),
        )(slot_source, table, doc_lengths, queries, keys, values)

    return jax.shard_map(
        local,
        mesh=mesh,
        in_specs=(P(("ctx", "head"), None), P("ctx", None), P("ctx", None), P(), P()),
        out_specs=P("ctx", "head"),
        check_vma=False,
    )
```

```python
import functools
import math

import jax
import jax.numpy as jnp
from jax import lax
from jax.experimental import pallas as pl
from jax.experimental.pallas import tpu as pltpu
from jax.sharding import PartitionSpec as P

HD = 128
GROUP = 8
DOC_MAX = 2048
MASKED = -1e30
CUTS = 2
MESH = pl.DeviceIdType.MESH


def turn(t, n):
    side = (n - t + 1) // 2
    return jnp.where((n - t) % 2 == 1, side, n - side)


def kernel(
    nctx, nhead, win, chunk,
    slots, table, lengths, q_ref, k_ref, v_ref, o_ref,
    qbuf, kvwin, bias, obuf, sbuf, rbuf, chosen, pick,
    own_sem, q_send, q_recv, kv_send, kv_recv, f_send, f_recv, o_send, o_recv, token,
):
    ctx = lax.axis_index("ctx")
    head = lax.axis_index("head")
    piece, width = q_ref.shape[0], q_ref.shape[1] // nhead
    rows = k_ref.shape[0]
    count = rows // piece
    heads = width // HD
    deep = nctx // 4
    z, xh, core = ctx // 4, lax.rem(ctx // 2, 2), lax.rem(ctx, 2)

    def along(distance):
        return (lax.rem(z + distance + deep, deep) * 4 + xh * 2 + core, head)

    above = along(1)
    opposite = (z * 4 + (1 - xh) * 2 + core, head)
    sibling = (z * 4 + xh * 2 + 1 - core, head)

    barrier = pltpu.get_barrier_semaphore()
    near = [along(1), along(-1), along(2), along(-2), opposite, sibling]
    near.append((z * 4 + (1 - xh) * 2 + 1 - core, head))
    for peer in near:
        pl.semaphore_signal(barrier, device_id=peer, device_id_type=MESH)

    @pl.loop(1, nhead)
    def _(t):
        pl.semaphore_signal(barrier, device_id=(ctx, lax.rem(head + t, nhead)), device_id_type=MESH)

    pl.semaphore_wait(barrier, nhead - 1 + len(near))

    kv_cols = pl.ds(pl.multiple_of(((head * heads) // GROUP) * HD, HD), HD)

    cut = rows // CUTS
    parts = range(2 * CUTS)

    def part(n, step):
        return kvwin.at[n // CUTS, pl.ds(pl.multiple_of((step * 2 + core) * rows + n % CUTS * cut, cut), cut)]

    def block(n):
        return (k_ref, v_ref)[n // CUTS].at[pl.ds(n % CUTS * cut, cut), kv_cols]

    def own_copy(n):
        return pltpu.make_async_copy(block(n), part(n, 4), own_sem.at[n])

    routes = [
        (above, None, 2),
        (above, 2, 0),
        (opposite, 2, 1 + 2 * xh),
        (opposite, (1 - xh) * 4, 3 - 2 * xh),
    ]

    def kv_copy(i, n):
        to, source, target = routes[i]
        src = block(n) if source is None else part(n, source)
        return pltpu.make_async_remote_copy(
            src_ref=src,
            dst_ref=part(n, target),
            send_sem=kv_send.at[i, n],
            recv_sem=kv_recv.at[i, n],
            device_id=to,
            device_id_type=MESH,
        )

    given = [4, 2, 0, 3 - 2 * xh, 1 + 2 * xh]

    def pass_copy(i, n):
        where = part(n, given[i])
        return pltpu.make_async_remote_copy(
            src_ref=where,
            dst_ref=where,
            send_sem=f_send.at[i, n],
            recv_sem=f_recv.at[i, n],
            device_id=sibling,
            device_id_type=MESH,
        )

    for n in parts:
        kv_copy(0, n).start()
    for n in parts:
        own_copy(n).start()

    def q_copy(t):
        peer = lax.rem(head + t, nhead)
        return pltpu.make_async_remote_copy(
            src_ref=q_ref.at[:, pl.ds(pl.multiple_of(peer * width, width), width)],
            dst_ref=qbuf.at[head],
            send_sem=q_send.at[t],
            recv_sem=q_recv.at[t],
            device_id=(ctx, peer),
            device_id_type=MESH,
        )

    @pl.loop(1, nhead)
    def _(t):
        q_copy(t).start()

    q_own = pltpu.make_async_copy(
        q_ref.at[:, pl.ds(pl.multiple_of(head * width, width), width)], qbuf.at[head], own_sem.at[2 * CUTS]
    )
    q_own.start()

    for i, distance in enumerate((1, -1, 2, -2)):
        pl.semaphore_signal(token.at[i], device_id=along(distance), device_id_type=MESH)

    lanes = lax.broadcasted_iota(jnp.int32, table.shape, 1) % count
    found = jnp.where(table[...] == ctx * count + lanes, lanes, 0)
    shift = count // 2
    while shift:
        found = found + pltpu.roll(found, table.shape[1] - shift, 1)
        shift //= 2
    chosen[...] = found
    pick_copy = pltpu.make_async_copy(chosen, pick, own_sem.at[2 * CUTS + 1])
    pick_copy.start()
    across = table.shape[1] // count

    keys = (win + 1) * rows
    for lower in range(0, rows, chunk):
        line = lower + lax.broadcasted_iota(jnp.int32, (chunk, 1), 0)
        position = ctx * rows + line
        start = jnp.zeros((chunk, 1), jnp.int32)
        end = jnp.int32(0)
        for j in range(lengths.shape[0]):
            end = end + lengths[j]
            start = jnp.where(position >= end, end, start)
        start = start - (ctx - win) * rows
        for col in range(0, keys, rows):
            at = col + lax.broadcasted_iota(jnp.int32, (chunk, rows), 1)
            allowed = (at >= start) & (at <= win * rows + line)
            bias[lower : lower + chunk, col : col + rows] = jnp.where(allowed, 0.0, MASKED)

    for n in parts:
        own_copy(n).wait()
        pass_copy(0, n).start()
    for n in parts:
        kv_copy(0, n).wait_recv()
        kv_copy(1, n).start()
        kv_copy(2, n).start()
        pass_copy(1, n).start()
    for i in range(4):
        pl.semaphore_wait(token.at[i], 1)
    for i, distance in enumerate((2, -2)):
        pl.semaphore_signal(token.at[4 + i], device_id=along(distance), device_id_type=MESH)
    for n in parts:
        kv_copy(1, n).wait_recv()
        kv_copy(3, n).start()
        pass_copy(2, n).start()
    for i in (2, 3):
        for n in parts:
            kv_copy(i, n).wait_recv()
            pass_copy(i + 1, n).start()
    q_own.wait()

    @pl.loop(1, nhead)
    def _(t):
        q_copy(t).wait_recv()

    for i in range(5):
        for n in parts:
            pass_copy(i, n).wait_recv()

    for i in range(2):
        pl.semaphore_wait(token.at[4 + i], 1)
    pick_copy.wait()
    seen = pl.ds(pl.multiple_of(core * rows, rows), keys)
    factor = math.log2(math.e) / HD**0.5

    def o_copy(h, t):
        owner = lax.rem(ctx + t, nctx)
        return pltpu.make_async_remote_copy(
            src_ref=sbuf.at[h, owner],
            dst_ref=rbuf.at[h, ctx],
            send_sem=o_send.at[h],
            recv_sem=o_recv.at[h],
            device_id=(owner, head),
            device_id_type=MESH,
        )

    @pl.loop(0, heads)
    def _(h):
        cols = pl.ds(pl.multiple_of(h * HD, HD), HD)
        for lower in range(0, rows, chunk):
            pieces = pl.ds(lower // piece, chunk // piece)
            query = qbuf[pieces, :, cols].reshape(chunk, HD)
            score = lax.dot_general(
                query, kvwin[0, seen], (((1,), (1,)), ((), ())), preferred_element_type=jnp.float32
            )
            score = score + bias[lower : lower + chunk, :]
            peak = jnp.max(score, axis=-1, keepdims=True)
            weight = jnp.exp2((score - peak) * factor)
            total = jnp.sum(weight, axis=-1, keepdims=True)
            mixed = jnp.dot(
                weight.astype(jnp.bfloat16), kvwin[1, seen], preferred_element_type=jnp.float32
            )
            mixed = mixed * (1.0 / total)
            obuf[h, pieces] = mixed.astype(jnp.bfloat16).reshape(chunk // piece, piece, HD)

        @pl.loop(0, nctx)
        def _(owner):
            sbuf[h, owner] = obuf[h, pick[owner // across, owner % across * count]]

        @pl.loop(1, nctx)
        def _(t):
            o_copy(h, turn(t, nctx)).start()

        rbuf[h, ctx] = sbuf[h, ctx]

    def o_waits(buffer, sem):
        for h in range(heads):
            moved = buffer.at[h, pl.ds(0, nctx - 1)]
            pltpu.make_async_copy(moved, moved, sem.at[h]).wait()

    o_waits(rbuf, o_recv)
    for h in range(heads):
        for place in range(count):
            source = slots[ctx * count + place] // count
            o_ref[place * piece : (place + 1) * piece, h * HD : (h + 1) * HD] = rbuf[h, source]

    o_waits(sbuf, o_send)

    @pl.loop(1, nhead)
    def _(t):
        q_copy(t).wait_send()

    for n in parts:
        for i in range(4):
            kv_copy(i, n).wait_send()
        for i in range(5):
            pass_copy(i, n).wait_send()


def solution(mesh):
    nctx, nhead = mesh.shape["ctx"], mesh.shape["head"]

    def local(queries, keys, values, doc_lengths, slot_source):
        piece, width = queries.shape[0], queries.shape[1] // nhead
        rows = keys.shape[0]
        heads = width // HD
        win = DOC_MAX // rows
        chunk = min(128, rows)
        table = slot_source.reshape(-1, min(128, slot_source.shape[0]))
        dma = pltpu.SemaphoreType.DMA
        return pl.pallas_call(
            functools.partial(kernel, nctx, nhead, win, chunk),
            out_shape=jax.ShapeDtypeStruct((rows, width), jnp.bfloat16),
            in_specs=[
                pl.BlockSpec(memory_space=pltpu.SMEM),
                pl.BlockSpec(memory_space=pltpu.VMEM),
                pl.BlockSpec(memory_space=pltpu.SMEM),
            ]
            + [pl.BlockSpec(memory_space=pl.ANY)] * 3,
            out_specs=pl.BlockSpec(memory_space=pltpu.VMEM),
            scratch_shapes=[
                pltpu.VMEM((rows // piece, piece, width), jnp.bfloat16),
                pltpu.VMEM((2, (win + 2) * rows, HD), jnp.bfloat16),
                pltpu.VMEM((rows, (win + 1) * rows), jnp.float32),
                pltpu.VMEM((heads, rows // piece, piece, HD), jnp.bfloat16),
                pltpu.VMEM((heads, nctx, piece, HD), jnp.bfloat16),
                pltpu.VMEM((heads, nctx, piece, HD), jnp.bfloat16),
                pltpu.VMEM(table.shape, jnp.int32),
                pltpu.SMEM(table.shape, jnp.int32),
                dma((2 * CUTS + 2,)),
                dma((nhead,)),
                dma((nhead,)),
                dma((4, 2 * CUTS)),
                dma((4, 2 * CUTS)),
                dma((5, 2 * CUTS)),
                dma((5, 2 * CUTS)),
                dma((heads,)),
                dma((heads,)),
                pltpu.SemaphoreType.REGULAR((6,)),
            ],
            compiler_params=pltpu.CompilerParams(
                collective_id=0, has_side_effects=True, vmem_limit_bytes=56 * 2**20
            ),
        )(slot_source, table, doc_lengths, queries, keys, values)

    return jax.shard_map(
        local,
        mesh=mesh,
        in_specs=(P(("ctx", "head"), None), P("ctx", None), P("ctx", None), P(), P()),
        out_specs=P("ctx", "head"),
        check_vma=False,
    )
```
